512 devices in a mesh: dp: 128 (over y, z, core), shard: 4 (over x).
Axes of the slice: x: 4, y: 8, z: 8, core: 2. Of those that a mesh axis runs over, the one named last changes fastest.
Arguments:
- acts: bfloat16 [131072, 1792], P('dp', 'shard'), may hold values from -6 to 6
- grad_out: bfloat16 [131072, 3584], P('dp', 'shard'), may hold values from -0.016479492 to 0.016479492
- projector: bfloat16 [1792, 256], P('shard'), may hold values from -6 to 6
- moment: bfloat16 [256, 3584], P(None, 'shard'), may hold values from -4 to 4
- second: bfloat16 [256, 3584], P(None, 'shard'), may hold values from 0.29882812 to 3
Outputs:
- new_projector: bfloat16 [1792, 256], P('shard')
- new_moment: bfloat16 [256, 3584], P(None, 'shard')
- new_second: bfloat16 [256, 3584], P(None, 'shard')
- weight_update: bfloat16 [1792, 3584], P('dp', 'shard')
The draws below stay inside these ranges and needn't reach their ends.
All inputs are finite; a program needn't handle non-finite values.
Results may differ from the reference program's by a relative error of at most 0.0055.
Values may be sent and summed in bfloat16 or wider, within the bound.
A program may use at most 64 MiB of HBM per device.

```python
import math
import jax
import jax.numpy as jnp
from jax import lax

D = 1792
F = 3584
RANK = 256
TOKENS = 131072


def block_levels(key, shape, cuts, smallest, high):
    def one(dim, parts):
        draws = jax.random.uniform(jax.random.fold_in(jax.random.fold_in(key, 6), dim), (parts,), jnp.float32, smallest / len(cuts), high / len(cuts))
        return jnp.repeat(jnp.exp(draws), shape[dim] // parts).reshape((-1,) + (1,) * (len(shape) - dim - 1))

    loudness = one(*cuts[0])
    for cut in cuts[1:]:
        loudness = loudness * one(*cut)
    return loudness


def scatter_about(own_key, shape, scale, limit, cuts=(), dtype=jnp.bfloat16):
    drawn = scale * jax.random.normal(own_key, shape, jnp.float32)
    if cuts:
        drawn = drawn * block_levels(own_key, shape, cuts, -0.22, 0.18)
    return jnp.clip(drawn, -limit, limit).astype(dtype)


def setup_inputs(seed: int = 0) -> dict:
    key_list = jax.random.split(jax.random.key(seed), 6)
    return {
        "acts": scatter_about(key_list[0], (TOKENS, D), 1.0, 6.0, ((0, 128), (1, 4))),
        "grad_out": scatter_about(key_list[1], (TOKENS, F), (TOKENS ** -0.5), 0.016479492, ((0, 128), (1, 4))),
        "projector": scatter_about(key_list[2], (D, RANK), 1.0, 6.0, ((0, 4),)),
        "moment": scatter_about(key_list[3], (RANK, F), 0.5, 4.0, ((1, 4),)),
        "second": jnp.clip(jnp.exp(math.log(3.0) - 2.306499 * jax.random.uniform(key_list[4], (RANK, F), jnp.float32) ** block_levels(key_list[4], (RANK, F), ((1, 4),), -0.2, 0.2)), 0.29882812, 3.0).astype(jnp.bfloat16),
    }


def reference(acts, grad_out, projector, moment, second):
    inv_width = 1.0 / D ** 0.5
    proj_acts = (jnp.dot(acts, projector, preferred_element_type=jnp.float32) * inv_width).astype(jnp.bfloat16)
    proj_grad = jnp.dot(proj_acts.T, grad_out, preferred_element_type=jnp.float32)
    proj_low = proj_grad.astype(jnp.bfloat16)
    token_scores = jnp.dot(grad_out, proj_low.T, preferred_element_type=jnp.float32).astype(jnp.bfloat16)
    subspace = jnp.dot(acts.T, token_scores, preferred_element_type=jnp.float32)
    gram_matrix = jnp.dot(subspace.T, subspace, precision=lax.Precision.HIGHEST, preferred_element_type=jnp.float32)
    mean_square = jnp.trace(gram_matrix) / (D * RANK) + 1e-06
    cubic = jnp.dot(subspace, gram_matrix, precision=lax.Precision.HIGHEST, preferred_element_type=jnp.float32)
    new_projector = ((1.5 * subspace - 0.5 * cubic / (mean_square * D)) / jnp.sqrt(mean_square)).astype(jnp.bfloat16)
    moment_f = 0.9 * moment.astype(jnp.float32) + 0.1 * proj_grad
    second_f = 0.95 * second.astype(jnp.float32) + 0.05 * proj_grad * proj_grad
    first_fix = 1.0 - 0.9 ** 20
    second_fix = 1.0 - 0.95 ** 20
    direction = (moment_f / first_fix / (jnp.sqrt(second_f / second_fix) + 1e-08)).astype(jnp.bfloat16)
    weight_update = (jnp.dot(projector, direction, preferred_element_type=jnp.float32) / RANK ** 0.5).astype(jnp.bfloat16)
    return (new_projector, moment_f.astype(jnp.bfloat16), second_f.astype(jnp.bfloat16), weight_update)
```

```python
import functools

import jax
import jax.numpy as jnp
from jax import lax
from jax.experimental import pallas as pl
from jax.experimental.pallas import tpu as pltpu
from jax.sharding import PartitionSpec as P

D = 1792
F = 3584
RANK = 256
NX, NY, NZ = 4, 8, 8
HALF = RANK // 2
STRIP = HALF // NY
MESH = pl.DeviceIdType.MESH
F32 = jnp.float32
BF16 = jnp.bfloat16


def dot_nt(a, b, precision=None):
    return lax.dot_general(
        a, b, (((1,), (1,)), ((), ())), precision=precision, preferred_element_type=F32
    )


def dot_nn(a, b, precision=None):
    return lax.dot_general(
        a, b, (((1,), (0,)), ((), ())), precision=precision, preferred_element_type=F32
    )


def step_kernel(
    acts, grad_hbm, proj, low_out, new_out, rows_out,
    grad, pt, rows, load_sem,
    xs, xr, xg,
    ys, yr, yg,
    l1, c1, h1, s1, r1, q1, g1,
    l2, c2, h2, s2, r2, q2, g2,
    gr, gf,
    xsend, xrecv, dsend, drecv,
):
    dp, x = lax.axis_index("dp"), lax.axis_index("shard")
    core = lax.rem(dp, 2)
    z = lax.rem(lax.div(dp, 2), NZ)
    y = lax.div(dp, 2 * NZ)
    other = 1 - core
    pos1 = y * other + z * core
    pos2 = y * core + z * other

    def on_x(j):
        return (dp, lax.rem(x + j, NX))

    def on_first(j):
        return ((lax.rem(y + j * other, NY) * NZ + lax.rem(z + j * core, NZ)) * 2 + core, x)

    def on_second(j):
        return ((lax.rem(y + j * core, NY) * NZ + lax.rem(z + j * other, NZ)) * 2 + core, x)

    partner = (dp + 1 - 2 * core, x)
    x_order = (2, 1, 3)
    order = (4, 3, 5, 2, 6, 1, 7)
    pending = []

    def send(src, dst, send_sem, recv_sem, device):
        copy = pltpu.make_async_remote_copy(
            src_ref=src, dst_ref=dst, send_sem=send_sem, recv_sem=recv_sem,
            device_id=device, device_id_type=MESH,
        )
        copy.start()
        pending.append(copy)
        return copy

    barrier = pltpu.get_barrier_semaphore()
    peers = [on_x(j) for j in x_order] + [partner]
    peers += [on_first(j) for j in order] + [on_second(j) for j in order]
    for peer in peers:
        pl.semaphore_signal(barrier, inc=1, device_id=peer, device_id_type=MESH)

    load = pltpu.make_async_copy(grad_hbm, grad, load_sem)
    load.start()

    def eye(n, m, shift):
        r = lax.broadcasted_iota(jnp.int32, (n, m), 0)
        c = lax.broadcasted_iota(jnp.int32, (n, m), 1)
        return jnp.where(r + shift == c, 1.0, 0.0)

    own_block = D // NX
    count = D // (NY * NZ * 2)
    pt[...] = dot_nt(eye(RANK, RANK, 0).astype(BF16), proj[...]).astype(BF16)
    first_row = lax.rem(dp, own_block // count) * count
    rows[x] = dot_nn(eye(16, own_block, first_row).astype(BF16), proj[...]).astype(BF16)

    quarter = acts.shape[0] // NX

    def tokens(ref, q):
        return ref[pl.ds(pl.multiple_of(q * quarter, quarter), quarter), :]

    def x_exchange(slot, term, finish, s, r, g, barrier_wait):
        copies = []
        for j in x_order:
            s[j - 1] = term(lax.rem(x + j, NX)).astype(BF16)
            if barrier_wait and not copies:
                pl.semaphore_wait(barrier, len(peers))
            k = slot + j - 1
            copies.append(send(s.at[j - 1], r.at[j - 1], xsend.at[k], xrecv.at[k], on_x(j)))
        total = term(x)
        for copy, j in zip(copies, x_order):
            copy.wait_recv()
        for j in x_order:
            total = total + r[j - 1].astype(F32)
        g[x] = finish(total).astype(BF16)
        gathers = {}
        for j in x_order:
            k = slot + 3 + j - 1
            gathers[j] = send(g.at[x], g.at[x], xsend.at[k], xrecv.at[k], on_x(j))
        return gathers

    def x_contract(g, gathers, other_ref):
        total = dot_nn(g[x], tokens(other_ref, x))
        for j in (1, 3, 2):
            gathers[j].wait_recv()
            q = lax.rem(x + NX - j, NX)
            total = total + dot_nn(g[q], tokens(other_ref, q))
        return total

    def plane_sum(slot, local, l, c, h, s, r, q, g):
        l[0] = local[:HALF]
        l[1] = local[HALF:]
        swap = send(l.at[other], c, dsend.at[slot], drecv.at[slot], partner)
        swap.wait_recv()
        for i in range(NY):
            strip = l[core, i * STRIP:(i + 1) * STRIP, :] + c[i * STRIP:(i + 1) * STRIP, :]
            h[i] = strip
            s[i] = strip.astype(s.dtype)
        copies = []
        for j in order:
            k = slot + j
            copies.append(
                send(s.at[lax.rem(pos1 + j, NY)], r.at[j - 1], dsend.at[k], drecv.at[k], on_first(j))
            )
        for copy in copies:
            copy.wait_recv()
        total = h[pos1]
        for j in range(1, NY):
            total = total + r[j - 1].astype(F32)
        q[pos2] = total.astype(q.dtype)
        copies = []
        for j in order:
            k = slot + 7 + j
            copies.append(send(q.at[pos2], q.at[pos2], dsend.at[k], drecv.at[k], on_second(j)))
        for copy in copies:
            copy.wait_recv()
        total = q[0].astype(F32)
        for j in range(1, NZ):
            total = total + q[j].astype(F32)
        g[core, pos1] = total.astype(g.dtype)
        copies = []
        for j in order:
            k = slot + 14 + j
            copies.append(
                send(g.at[core, pos1], g.at[core, pos1], dsend.at[k], drecv.at[k], on_first(j))
            )
        for copy in copies:
            copy.wait_recv()
        send(g.at[core], g.at[core], dsend.at[slot + 22], drecv.at[slot + 22], partner).wait_recv()
        return g[...].reshape(RANK, local.shape[1])

    inv_width = 1.0 / D**0.5
    gathers = x_exchange(
        0, lambda q: dot_nt(pt[...], tokens(acts, q)), lambda v: v * inv_width, xs, xr, xg, True
    )
    row_copies = []
    for j in x_order:
        k = 12 + j - 1
        row_copies.append(send(rows.at[x], rows.at[x], xsend.at[k], xrecv.at[k], on_x(j)))
    load.wait()
    low = plane_sum(0, x_contract(xg, gathers, grad), l1, c1, h1, s1, r1, q1, g1)
    low_out[...] = low
    gathers = x_exchange(
        6, lambda q: dot_nt(low_out[...], tokens(grad, q)), lambda v: v, ys, yr, yg, False
    )
    for copy in row_copies:
        copy.wait_recv()
    rows_out[...] = rows[...]
    sub = plane_sum(23, x_contract(yg, gathers, acts), l2, c2, h2, s2, r2, q2, g2)

    high = lax.Precision.HIGHEST
    mine = g2[core].reshape(HALF, own_block)
    gr[x] = dot_nt(mine, sub, high)
    copies = []
    for j in x_order:
        k = 15 + j - 1
        copies.append(send(gr.at[x], gr.at[x], xsend.at[k], xrecv.at[k], on_x(j)))
    for copy in copies:
        copy.wait_recv()
    gf[core] = gr[0] + gr[1] + gr[2] + gr[3]
    send(gf.at[core], gf.at[core], dsend.at[46], drecv.at[46], partner).wait_recv()
    gram = gf[...].reshape(RANK, RANK)
    trace = jnp.sum(gram * eye(RANK, RANK, 0), axis=(0, 1), keepdims=True)
    mean_square = trace / (D * RANK) + 1e-06
    cubic = dot_nn(gram, sub, high)
    new = (1.5 * sub - 0.5 * cubic / (mean_square * D)) / jnp.sqrt(mean_square)
    new_out[...] = new.astype(BF16)
    for copy in pending:
        copy.wait_send()


def fused(acts, grad_out, projector):
    tokens, own = acts.shape
    wide = grad_out.shape[1]
    quarter = tokens // NX

    def plane(width, part, gathered):
        return [
            pltpu.VMEM((2, HALF, width), F32),
            pltpu.VMEM((HALF, width), F32),
            pltpu.VMEM((NY, STRIP, width), F32),
            pltpu.VMEM((NY, STRIP, width), BF16),
            pltpu.VMEM((NY - 1, STRIP, width), BF16),
            pltpu.VMEM((NZ, STRIP, width), part),
            pltpu.VMEM((2, NY, STRIP, width), gathered),
        ]

    def cross():
        return [
            pltpu.VMEM((NX - 1, RANK, quarter), BF16),
            pltpu.VMEM((NX - 1, RANK, quarter), BF16),
            pltpu.VMEM((NX, RANK, quarter), BF16),
        ]

    vmem = pl.BlockSpec(memory_space=pltpu.VMEM)
    return pl.pallas_call(
        step_kernel,
        out_shape=(
            jax.ShapeDtypeStruct((RANK, wide), BF16),
            jax.ShapeDtypeStruct((RANK, own), BF16),
            jax.ShapeDtypeStruct((NX, 16, RANK), BF16),
        ),
        in_specs=[vmem, pl.BlockSpec(memory_space=pl.ANY), vmem],
        out_specs=(vmem, vmem, vmem),
        scratch_shapes=[
            pltpu.VMEM((tokens, wide), BF16),
            pltpu.VMEM((RANK, own), BF16),
            pltpu.VMEM((NX, 16, RANK), BF16),
            pltpu.SemaphoreType.DMA,
            *cross(),
            *cross(),
            *plane(wide, BF16, BF16),
            *plane(own, F32, F32),
            pltpu.VMEM((NX, HALF, RANK), F32),
            pltpu.VMEM((2, HALF, RANK), F32),
            pltpu.SemaphoreType.DMA((18,)),
            pltpu.SemaphoreType.DMA((18,)),
            pltpu.SemaphoreType.DMA((47,)),
            pltpu.SemaphoreType.DMA((47,)),
        ],
        compiler_params=pltpu.CompilerParams(
            collective_id=0, has_side_effects=True, vmem_limit_bytes=48 * 1024 * 1024
        ),
    )(acts, grad_out, projector)


def shards(acts, grad_out, projector, moment, second):
    low, new_t, rows = fused(acts, grad_out, projector)
    proj_grad = low.astype(F32)
    moment_f = 0.9 * moment.astype(F32) + 0.1 * proj_grad
    second_f = 0.95 * second.astype(F32) + 0.05 * proj_grad * proj_grad
    first_fix = 1.0 - 0.9**20
    second_fix = 1.0 - 0.95**20
    direction = (moment_f / first_fix / (jnp.sqrt(second_f / second_fix) + 1e-08)).astype(BF16)
    row_count = D // lax.axis_size("dp")
    owner = lax.axis_index("dp") // (D // NX // row_count)
    own_rows = lax.dynamic_index_in_dim(rows, owner, 0, keepdims=False)[:row_count]
    weight_update = (
        jnp.dot(own_rows, direction, preferred_element_type=F32) / RANK**0.5
    ).astype(BF16)
    return new_t.T, moment_f.astype(BF16), second_f.astype(BF16), weight_update


def solution(mesh):
    in_specs = (
        P("dp", "shard"),
        P("dp", "shard"),
        P("shard", None),
        P(None, "shard"),
        P(None, "shard"),
    )
    out_specs = (P("shard", None), P(None, "shard"), P(None, "shard"), P("dp", "shard"))
    return jax.shard_map(shards, mesh=mesh, in_specs=in_specs, out_specs=out_specs, check_vma=False)
```

```python
import jax
import jax.numpy as jnp
from jax import lax
from jax.experimental import pallas as pl
from jax.experimental.pallas import tpu as pltpu
from jax.sharding import PartitionSpec as P

D = 1792
F = 3584
RANK = 256
NX, NY, NZ = 4, 8, 8
CHUNKS = 2
CHUNK = RANK // CHUNKS
HALF = CHUNK // 2
STRIP = HALF // NY
MESH = pl.DeviceIdType.MESH
F32 = jnp.float32
BF16 = jnp.bfloat16


def dot_nt(a, b, precision=None):
    return lax.dot_general(
        a, b, (((1,), (1,)), ((), ())), precision=precision, preferred_element_type=F32
    )


def dot_nn(a, b, precision=None):
    return lax.dot_general(
        a, b, (((1,), (0,)), ((), ())), precision=precision, preferred_element_type=F32
    )


def step_kernel(
    acts_hbm, grad_hbm, proj_hbm, moment_hbm, second_hbm,
    low_hbm, new_out, update_out,
    acts, grad, proj, moment, second, pt, rows, low,
    xs, xr, xg, ys, yr, yg,
    l1, c1, h1, s1, r1, q1, g1,
    l2, c2, h2, s2, r2, q2, g2,
    gr, gf,
    load, xsend, xrecv, dsend, drecv,
):
    dp, x = lax.axis_index("dp"), lax.axis_index("shard")
    core = lax.rem(dp, 2)
    z = lax.rem(lax.div(dp, 2), NZ)
    y = lax.div(dp, 2 * NZ)
    other = 1 - core
    pos1 = y * other + z * core
    pos2 = y * core + z * other

    def on_x(j):
        return (dp, lax.rem(x + j, NX))

    def on_first(j):
        return ((lax.rem(y + j * other, NY) * NZ + lax.rem(z + j * core, NZ)) * 2 + core, x)

    def on_second(j):
        return ((lax.rem(y + j * core, NY) * NZ + lax.rem(z + j * other, NZ)) * 2 + core, x)

    partner = (dp + 1 - 2 * core, x)
    x_order = (2, 1, 3)
    order = (4, 3, 5, 2, 6, 1, 7)
    pending = []

    def send(src, dst, send_sem, recv_sem, device):
        copy = pltpu.make_async_remote_copy(
            src_ref=src, dst_ref=dst, send_sem=send_sem, recv_sem=recv_sem,
            device_id=device, device_id_type=MESH,
        )
        copy.start()
        pending.append(copy)
        return copy

    barrier = pltpu.get_barrier_semaphore()
    peers = [on_x(j) for j in x_order] + [partner]
    peers += [on_first(j) for j in order] + [on_second(j) for j in order]
    for peer in peers:
        pl.semaphore_signal(barrier, inc=1, device_id=peer, device_id_type=MESH)

    loads = []
    pairs = ((proj_hbm, proj), (acts_hbm, acts), (grad_hbm, grad), (moment_hbm, moment), (second_hbm, second))
    for i, (source, target) in enumerate(pairs):
        loads.append(pltpu.make_async_copy(source, target, load.at[i]))
        loads[-1].start()

    def eye(n, m, shift):
        r = lax.broadcasted_iota(jnp.int32, (n, m), 0)
        c = lax.broadcasted_iota(jnp.int32, (n, m), 1)
        return jnp.where(r + shift == c, 1.0, 0.0)

    own_block = D // NX
    count = D // (NY * NZ * 2)
    quarter = grad.shape[0] // NX
    loads[0].wait()
    pt[...] = dot_nt(eye(RANK, RANK, 0).astype(BF16), proj[...]).astype(BF16)
    first_row = lax.rem(dp, own_block // count) * count
    rows[x] = dot_nn(eye(16, own_block, first_row).astype(BF16), proj[...]).astype(BF16)
    loads[1].wait()

    def span(q):
        return pl.ds(pl.multiple_of(q * quarter, quarter), quarter)

    done = {}

    def once(name, action):
        if name not in done:
            done[name] = action()

    def x_exchange(slot, term, finish, s, r, g):
        copies = []
        for j in x_order:
            s[j - 1] = term(lax.rem(x + j, NX)).astype(BF16)
            once("barrier", lambda: pl.semaphore_wait(barrier, len(peers)))
            k = slot + j - 1
            copies.append(send(s.at[j - 1], r.at[j - 1], xsend.at[k], xrecv.at[k], on_x(j)))
        total = term(x)
        yield
        for copy, j in zip(copies, x_order):
            copy.wait_recv()
            total = total + r[j - 1].astype(F32)
        g[x] = finish(total).astype(BF16)
        gathers = {}
        for j in x_order:
            k = slot + 3 + j - 1
            gathers[j] = send(g.at[x], g.at[x], xsend.at[k], xrecv.at[k], on_x(j))
        return gathers

    def x_contract(g, gathers, term):
        total = term(g[x], x)
        yield
        for j in (1, 3, 2):
            gathers[j].wait_recv()
            q = lax.rem(x + NX - j, NX)
            total = total + term(g[q], q)
        return total

    def plane_sum(slot, local, l, c, h, s, r, q, g):
        l[0] = local[:HALF]
        l[1] = local[HALF:]
        swap = send(l.at[other], c, dsend.at[slot], drecv.at[slot], partner)
        yield
        swap.wait_recv()
        for i in range(NY):
            strip = l[core, i * STRIP:(i + 1) * STRIP, :] + c[i * STRIP:(i + 1) * STRIP, :]
            h[i] = strip
            s[i] = strip.astype(s.dtype)
        copies = []
        for j in order:
            k = slot + j
            copies.append(
                send(s.at[lax.rem(pos1 + j, NY)], r.at[j - 1], dsend.at[k], drecv.at[k], on_first(j))
            )
        yield
        for copy in copies:
            copy.wait_recv()
        total = h[pos1]
        for j in range(1, NY):
            total = total + r[j - 1].astype(F32)
        q[pos2] = total.astype(q.dtype)
        copies = []
        for j in order:
            k = slot + 7 + j
            copies.append(send(q.at[pos2], q.at[pos2], dsend.at[k], drecv.at[k], on_second(j)))
        yield
        for copy in copies:
            copy.wait_recv()
        total = q[0].astype(F32)
        for j in range(1, NZ):
            total = total + q[j].astype(F32)
        g[core, pos1] = total.astype(g.dtype)
        copies = []
        for j in order:
            k = slot + 14 + j
            copies.append(
                send(g.at[core, pos1], g.at[core, pos1], dsend.at[k], drecv.at[k], on_first(j))
            )
        yield
        for copy in copies:
            copy.wait_recv()
        swap = send(g.at[core], g.at[core], dsend.at[slot + 22], drecv.at[slot + 22], partner)
        yield
        swap.wait_recv()

    inv_width = 1.0 / D**0.5
    row_copies = []
    updates = []

    def send_rows():
        for j in x_order:
            k = 12 * CHUNKS + j - 1
            row_copies.append(send(rows.at[x], rows.at[x], xsend.at[k], xrecv.at[k], on_x(j)))

    def wait_rows():
        for copy in row_copies:
            copy.wait_recv()

    def wait_states():
        loads[3].wait()
        loads[4].wait()

    def chain(i):
        part = slice(i * CHUNK, (i + 1) * CHUNK)
        gathers = yield from x_exchange(
            12 * i, lambda q: dot_nn(pt[part, :], acts[:, span(q)]), lambda v: v * inv_width,
            xs.at[i], xr.at[i], xg.at[i],
        )
        once("rows", send_rows)
        once("grad", loads[2].wait)
        local = yield from x_contract(xg.at[i], gathers, lambda v, q: dot_nn(v, grad[span(q), :]))
        bufs = [b.at[i] for b in (l1, c1, h1, s1, r1, q1, g1)]
        yield from plane_sum(46 * i, local, *bufs)
        low[i] = g1[i].reshape(CHUNK, grad.shape[1])
        store = pltpu.make_async_copy(low.at[i], low_hbm.at[pl.ds(i * CHUNK, CHUNK), :], load.at[5 + i])
        store.start()
        exchange = x_exchange(
            12 * i + 6, lambda q: dot_nt(low[i], grad[span(q), :]), lambda v: v,
            ys.at[i], yr.at[i], yg.at[i],
        )
        next(exchange)
        once("states", wait_states)
        once("wait_rows", wait_rows)
        step = low[i].astype(F32)
        moment_f = 0.9 * moment[part, :].astype(F32) + 0.1 * step
        second_f = 0.95 * second[part, :].astype(F32) + 0.05 * step * step
        first_fix = 1.0 - 0.9**20
        second_fix = 1.0 - 0.95**20
        direction = (moment_f / first_fix / (jnp.sqrt(second_f / second_fix) + 1e-08)).astype(BF16)
        mine = rows[lax.div(dp, own_block // count)]
        updates.append(dot_nn(mine[:, part], direction))
        yield
        gathers = yield from exchange
        local = yield from x_contract(yg.at[i], gathers, lambda v, q: dot_nt(v, acts[:, span(q)]))
        bufs = [b.at[i] for b in (l2, c2, h2, s2, r2, q2, g2)]
        yield from plane_sum(46 * i + 23, local, *bufs)
        store.wait()

    live = [chain(i) for i in range(CHUNKS)]
    while live:
        for one in list(live):
            try:
                next(one)
            except StopIteration:
                live.remove(one)

    high = lax.Precision.HIGHEST
    sub = g2[...].reshape(RANK, own_block)
    mine = g2[core].reshape(CHUNK, own_block)
    gr[x] = dot_nt(mine, sub, high).astype(BF16)
    copies = []
    for j in x_order:
        k = 12 * CHUNKS + 3 + j - 1
        copies.append(send(gr.at[x], gr.at[x], xsend.at[k], xrecv.at[k], on_x(j)))
    update_out[...] = (sum(updates) / RANK**0.5).astype(BF16)
    for copy in copies:
        copy.wait_recv()
    total = gr[0].astype(F32)
    for j in range(1, NX):
        total = total + gr[j].astype(F32)
    gf[core] = total
    k = 46 * CHUNKS
    send(gf.at[core], gf.at[core], dsend.at[k], drecv.at[k], partner).wait_recv()
    gram = gf[...].reshape(RANK, RANK)
    trace = jnp.sum(gram * eye(RANK, RANK, 0), axis=(0, 1), keepdims=True)
    mean_square = trace / (D * RANK) + 1e-06
    cubic = dot_nn(gram, sub, high)
    new = (1.5 * sub - 0.5 * cubic / (mean_square * D)) / jnp.sqrt(mean_square)
    new_out[...] = dot_nt(eye(own_block, own_block, 0).astype(BF16), new.astype(BF16)).astype(BF16)
    for copy in pending:
        copy.wait_send()


def fused(acts, grad_out, projector, moment, second):
    own, tokens = acts.shape
    wide = grad_out.shape[1]
    quarter = tokens // NX

    def plane(width, part, gathered):
        return [
            pltpu.VMEM((CHUNKS, 2, HALF, width), F32),
            pltpu.VMEM((CHUNKS, HALF, width), F32),
            pltpu.VMEM((CHUNKS, NY, STRIP, width), F32),
            pltpu.VMEM((CHUNKS, NY, STRIP, width), BF16),
            pltpu.VMEM((CHUNKS, NY - 1, STRIP, width), BF16),
            pltpu.VMEM((CHUNKS, NZ, STRIP, width), part),
            pltpu.VMEM((CHUNKS, 2, NY, STRIP, width), gathered),
        ]

    def cross():
        return [
            pltpu.VMEM((CHUNKS, NX - 1, CHUNK, quarter), BF16),
            pltpu.VMEM((CHUNKS, NX - 1, CHUNK, quarter), BF16),
            pltpu.VMEM((CHUNKS, NX, CHUNK, quarter), BF16),
        ]

    vmem = pl.BlockSpec(memory_space=pltpu.VMEM)
    anywhere = pl.BlockSpec(memory_space=pl.ANY)
    return pl.pallas_call(
        step_kernel,
        out_shape=(
            jax.ShapeDtypeStruct((RANK, wide), BF16),
            jax.ShapeDtypeStruct((own, RANK), BF16),
            jax.ShapeDtypeStruct((16, wide), BF16),
        ),
        in_specs=[anywhere] * 5,
        out_specs=(anywhere, vmem, vmem),
        scratch_shapes=[
            pltpu.VMEM((own, tokens), BF16),
            pltpu.VMEM((tokens, wide), BF16),
            pltpu.VMEM((own, RANK), BF16),
            pltpu.VMEM((RANK, wide), BF16),
            pltpu.VMEM((RANK, wide), BF16),
            pltpu.VMEM((RANK, own), BF16),
            pltpu.VMEM((NX, 16, RANK), BF16),
            pltpu.VMEM((CHUNKS, CHUNK, wide), BF16),
            *cross(),
            *cross(),
            *plane(wide, BF16, BF16),
            *plane(own, F32, F32),
            pltpu.VMEM((NX, CHUNK, RANK), BF16),
            pltpu.VMEM((2, CHUNK, RANK), F32),
            pltpu.SemaphoreType.DMA((5 + CHUNKS,)),
            pltpu.SemaphoreType.DMA((12 * CHUNKS + 6,)),
            pltpu.SemaphoreType.DMA((12 * CHUNKS + 6,)),
            pltpu.SemaphoreType.DMA((46 * CHUNKS + 1,)),
            pltpu.SemaphoreType.DMA((46 * CHUNKS + 1,)),
        ],
        compiler_params=pltpu.CompilerParams(
            collective_id=0, has_side_effects=True, vmem_limit_bytes=67043328
        ),
    )(acts, grad_out, projector, moment, second)


def shards(acts, grad_out, projector, moment, second):
    low, new_projector, update = fused(acts.T, grad_out, projector, moment, second)
    proj_grad = low.astype(F32)
    moment_f = 0.9 * moment.astype(F32) + 0.1 * proj_grad
    second_f = 0.95 * second.astype(F32) + 0.05 * proj_grad * proj_grad
    row_count = D // lax.axis_size("dp")
    return new_projector, moment_f.astype(BF16), second_f.astype(BF16), update[:row_count]


def solution(mesh):
    in_specs = (
        P("dp", "shard"),
        P("dp", "shard"),
        P("shard", None),
        P(None, "shard"),
        P(None, "shard"),
    )
    out_specs = (P("shard", None), P(None, "shard"), P(None, "shard"), P("dp", "shard"))
    return jax.shard_map(shards, mesh=mesh, in_specs=in_specs, out_specs=out_specs, check_vma=False)
```

```python
import jax
import jax.numpy as jnp
from jax import lax
from jax.experimental import pallas as pl
from jax.experimental.pallas import tpu as pltpu
from jax.sharding import PartitionSpec as P

D = 1792
F = 3584
RANK = 256
NX, NY, NZ = 4, 8, 8
CHUNKS = 2
CHUNK = RANK // CHUNKS
HALF = CHUNK // 2
STRIP = HALF // NY
MESH = pl.DeviceIdType.MESH
F32 = jnp.float32
BF16 = jnp.bfloat16


def dot_nt(a, b, precision=None):
    return lax.dot_general(
        a, b, (((1,), (1,)), ((), ())), precision=precision, preferred_element_type=F32
    )


def dot_nn(a, b, precision=None):
    return lax.dot_general(
        a, b, (((1,), (0,)), ((), ())), precision=precision, preferred_element_type=F32
    )


def step_kernel(
    acts_hbm, grad_hbm, proj_hbm, moment_hbm, second_hbm,
    low_hbm, new_out, update_out,
    acts, grad, proj, moment, second, pt, rows, low,
    xs, xr, xg, ys, yr, yg,
    h1, s1, r1, q1, g1,
    h2, s2, r2, q2, g2,
    gr, gf,
    load, xsend, xrecv, dsend, drecv,
):
    dp, x = lax.axis_index("dp"), lax.axis_index("shard")
    core = lax.rem(dp, 2)
    z = lax.rem(lax.div(dp, 2), NZ)
    y = lax.div(dp, 2 * NZ)
    other = 1 - core
    pos1 = y * other + z * core
    pos2 = y * core + z * other

    def on_x(j):
        return (dp, lax.rem(x + j, NX))

    def on_first(j):
        return ((lax.rem(y + j * other, NY) * NZ + lax.rem(z + j * core, NZ)) * 2 + core, x)

    def on_second(j):
        return ((lax.rem(y + j * core, NY) * NZ + lax.rem(z + j * other, NZ)) * 2 + core, x)

    def on_cross(j, axis):
        row = lax.rem(y + j * (1 - axis), NY)
        return ((row * NZ + lax.rem(z + j * axis, NZ)) * 2 + other, x)

    partner = (dp + 1 - 2 * core, x)
    x_order = (2, 1, 3)
    order = (4, 3, 5, 2, 6, 1, 7)
    pending = []

    def send(src, dst, send_sem, recv_sem, device):
        copy = pltpu.make_async_remote_copy(
            src_ref=src, dst_ref=dst, send_sem=send_sem, recv_sem=recv_sem,
            device_id=device, device_id_type=MESH,
        )
        copy.start()
        pending.append(copy)
        return copy

    barrier = pltpu.get_barrier_semaphore()
    peers = [on_x(j) for j in x_order] + [partner]
    peers += [on_first(j) for j in order] + [on_second(j) for j in order]
    peers += [on_cross(j, axis) for axis in (core, other) for j in order]
    for peer in peers:
        pl.semaphore_signal(barrier, inc=1, device_id=peer, device_id_type=MESH)

    loads = []
    pairs = ((proj_hbm, proj), (acts_hbm, acts), (grad_hbm, grad), (moment_hbm, moment), (second_hbm, second))
    for i, (source, target) in enumerate(pairs):
        loads.append(pltpu.make_async_copy(source, target, load.at[i]))
        loads[-1].start()

    def eye(n, m, shift):
        r = lax.broadcasted_iota(jnp.int32, (n, m), 0)
        c = lax.broadcasted_iota(jnp.int32, (n, m), 1)
        return jnp.where(r + shift == c, 1.0, 0.0)

    own_block = D // NX
    count = D // (NY * NZ * 2)
    quarter = grad.shape[0] // NX
    loads[0].wait()
    pt[...] = dot_nt(eye(RANK, RANK, 0).astype(BF16), proj[...]).astype(BF16)
    first_row = lax.rem(dp, own_block // count) * count
    rows[x] = dot_nn(eye(16, own_block, first_row).astype(BF16), proj[...]).astype(BF16)
    loads[1].wait()

    def span(q):
        return pl.ds(pl.multiple_of(q * quarter, quarter), quarter)

    done = {}

    def once(name, action):
        if name not in done:
            done[name] = action()

    def x_exchange(slot, term, finish, s, r, g):
        copies = []
        for j in x_order:
            s[j - 1] = term(lax.rem(x + j, NX)).astype(BF16)
            once("barrier", lambda: pl.semaphore_wait(barrier, len(peers)))
            k = slot + j - 1
            copies.append(send(s.at[j - 1], r.at[j - 1], xsend.at[k], xrecv.at[k], on_x(j)))
        total = term(x)
        yield
        for copy, j in zip(copies, x_order):
            copy.wait_recv()
            total = total + r[j - 1].astype(F32)
        g[x] = finish(total).astype(BF16)
        gathers = {}
        for j in x_order:
            k = slot + 3 + j - 1
            gathers[j] = send(g.at[x], g.at[x], xsend.at[k], xrecv.at[k], on_x(j))
        return gathers

    def x_contract(g, gathers, term):
        total = term(g[x], x)
        yield
        for j in (1, 3, 2):
            gathers[j].wait_recv()
            q = lax.rem(x + NX - j, NX)
            total = total + term(g[q], q)
        return total

    def plane_sum(slot, local, h, s, r, q, g):
        for half in range(2):
            for i in range(NY):
                first = half * HALF + i * STRIP
                strip = local[first:first + STRIP]
                s[half, i] = strip.astype(BF16)
                h[half, i] = strip
        copies = []
        at = y * core + z * other
        for j in order:
            k = slot + j
            source = s.at[core, lax.rem(pos1 + j, NY)]
            copies.append(send(source, r.at[j - 1], dsend.at[k], drecv.at[k], on_first(j)))
            k = slot + 22 + j
            source = s.at[other, lax.rem(at + j, NY)]
            copies.append(send(source, r.at[6 + j], dsend.at[k], drecv.at[k], on_cross(j, other)))
        k = slot
        copies.append(send(s.at[other, at], r.at[14], dsend.at[k], drecv.at[k], partner))
        yield
        for copy in copies:
            copy.wait_recv()
        total = h[core, pos1]
        for j in range(15):
            total = total + r[j].astype(F32)
        q[pos2] = total.astype(q.dtype)
        copies = []
        for j in order:
            k = slot + 7 + j
            copies.append(send(q.at[pos2], q.at[pos2], dsend.at[k], drecv.at[k], on_second(j)))
        yield
        for copy in copies:
            copy.wait_recv()
        total = q[0].astype(F32)
        for j in range(1, NZ):
            total = total + q[j].astype(F32)
        g[core, pos1] = total.astype(g.dtype)
        copies = []
        for j in order:
            k = slot + 14 + j
            copies.append(
                send(g.at[core, pos1], g.at[core, pos1], dsend.at[k], drecv.at[k], on_first(j))
            )
        yield
        for copy in copies:
            copy.wait_recv()
        swap = send(g.at[core], g.at[core], dsend.at[slot + 22], drecv.at[slot + 22], partner)
        yield
        swap.wait_recv()

    inv_width = 1.0 / D**0.5
    row_copies = []
    updates = []

    def send_rows():
        for j in x_order:
            k = 12 * CHUNKS + j - 1
            row_copies.append(send(rows.at[x], rows.at[x], xsend.at[k], xrecv.at[k], on_x(j)))

    def wait_rows():
        for copy in row_copies:
            copy.wait_recv()

    def wait_states():
        loads[3].wait()
        loads[4].wait()

    def chain(i):
        part = slice(i * CHUNK, (i + 1) * CHUNK)
        gathers = yield from x_exchange(
            12 * i, lambda q: dot_nn(pt[part, :], acts[:, span(q)]), lambda v: v * inv_width,
            xs.at[i], xr.at[i], xg.at[i],
        )
        once("rows", send_rows)
        once("grad", loads[2].wait)
        local = yield from x_contract(xg.at[i], gathers, lambda v, q: dot_nn(v, grad[span(q), :]))
        bufs = [b.at[i] for b in (h1, s1, r1, q1, g1)]
        yield from plane_sum(76 * i, local, *bufs)
        low[i] = g1[i].reshape(CHUNK, grad.shape[1])
        store = pltpu.make_async_copy(low.at[i], low_hbm.at[pl.ds(i * CHUNK, CHUNK), :], load.at[5 + i])
        store.start()
        exchange = x_exchange(
            12 * i + 6, lambda q: dot_nt(low[i], grad[span(q), :]), lambda v: v,
            ys.at[i], yr.at[i], yg.at[i],
        )
        next(exchange)
        once("states", wait_states)
        once("wait_rows", wait_rows)
        step = low[i].astype(F32)
        moment_f = 0.9 * moment[part, :].astype(F32) + 0.1 * step
        second_f = 0.95 * second[part, :].astype(F32) + 0.05 * step * step
        first_fix = 1.0 - 0.9**20
        second_fix = 1.0 - 0.95**20
        direction = (moment_f / first_fix / (jnp.sqrt(second_f / second_fix) + 1e-08)).astype(BF16)
        mine = rows[lax.div(dp, own_block // count)]
        updates.append(dot_nn(mine[:, part], direction))
        yield
        gathers = yield from exchange
        local = yield from x_contract(yg.at[i], gathers, lambda v, q: dot_nt(v, acts[:, span(q)]))
        bufs = [b.at[i] for b in (h2, s2, r2, q2, g2)]
        yield from plane_sum(76 * i + 38, local, *bufs)
        store.wait()

    live = [chain(i) for i in range(CHUNKS)]
    while live:
        for one in list(live):
            try:
                next(one)
            except StopIteration:
                live.remove(one)

    sub = g2[...].reshape(RANK, own_block)
    low_sub = sub.astype(BF16)
    mine = g2[core].reshape(CHUNK, own_block).astype(BF16)
    gr[x] = dot_nt(mine, low_sub).astype(BF16)
    copies = []
    for j in x_order:
        k = 12 * CHUNKS + 3 + j - 1
        copies.append(send(gr.at[x], gr.at[x], xsend.at[k], xrecv.at[k], on_x(j)))
    update_out[...] = (sum(updates) / RANK**0.5).astype(BF16)
    for copy in copies:
        copy.wait_recv()
    total = gr[0].astype(F32)
    for j in range(1, NX):
        total = total + gr[j].astype(F32)
    gf[core] = total
    k = 76 * CHUNKS
    send(gf.at[core], gf.at[core], dsend.at[k], drecv.at[k], partner).wait_recv()
    gram = gf[...].reshape(RANK, RANK)
    trace = jnp.sum(gram * eye(RANK, RANK, 0), axis=(0, 1), keepdims=True)
    mean_square = trace / (D * RANK) + 1e-06
    cubic = dot_nn(gram.astype(BF16), low_sub)
    new = (1.5 * sub - 0.5 * cubic / (mean_square * D)) / jnp.sqrt(mean_square)
    new_out[...] = dot_nt(eye(own_block, own_block, 0).astype(BF16), new.astype(BF16)).astype(BF16)
    for copy in pending:
        copy.wait_send()


def fused(acts, grad_out, projector, moment, second):
    own, tokens = acts.shape
    wide = grad_out.shape[1]
    quarter = tokens // NX

    def plane(width, part, gathered):
        return [
            pltpu.VMEM((CHUNKS, 2, NY, STRIP, width), F32),
            pltpu.VMEM((CHUNKS, 2, NY, STRIP, width), BF16),
            pltpu.VMEM((CHUNKS, 2 * NY - 1, STRIP, width), BF16),
            pltpu.VMEM((CHUNKS, NZ, STRIP, width), part),
            pltpu.VMEM((CHUNKS, 2, NY, STRIP, width), gathered),
        ]

    def cross():
        return [
            pltpu.VMEM((CHUNKS, NX - 1, CHUNK, quarter), BF16),
            pltpu.VMEM((CHUNKS, NX - 1, CHUNK, quarter), BF16),
            pltpu.VMEM((CHUNKS, NX, CHUNK, quarter), BF16),
        ]

    vmem = pl.BlockSpec(memory_space=pltpu.VMEM)
    anywhere = pl.BlockSpec(memory_space=pl.ANY)
    return pl.pallas_call(
        step_kernel,
        out_shape=(
            jax.ShapeDtypeStruct((RANK, wide), BF16),
            jax.ShapeDtypeStruct((own, RANK), BF16),
            jax.ShapeDtypeStruct((16, wide), BF16),
        ),
        in_specs=[anywhere] * 5,
        out_specs=(anywhere, vmem, vmem),
        scratch_shapes=[
            pltpu.VMEM((own, tokens), BF16),
            pltpu.VMEM((tokens, wide), BF16),
            pltpu.VMEM((own, RANK), BF16),
            pltpu.VMEM((RANK, wide), BF16),
            pltpu.VMEM((RANK, wide), BF16),
            pltpu.VMEM((RANK, own), BF16),
            pltpu.VMEM((NX, 16, RANK), BF16),
            pltpu.VMEM((CHUNKS, CHUNK, wide), BF16),
            *cross(),
            *cross(),
            *plane(wide, BF16, BF16),
            *plane(own, F32, F32),
            pltpu.VMEM((NX, CHUNK, RANK), BF16),
            pltpu.VMEM((2, CHUNK, RANK), F32),
            pltpu.SemaphoreType.DMA((5 + CHUNKS,)),
            pltpu.SemaphoreType.DMA((12 * CHUNKS + 6,)),
            pltpu.SemaphoreType.DMA((12 * CHUNKS + 6,)),
            pltpu.SemaphoreType.DMA((76 * CHUNKS + 1,)),
            pltpu.SemaphoreType.DMA((76 * CHUNKS + 1,)),
        ],
        compiler_params=pltpu.CompilerParams(
            collective_id=0, has_side_effects=True, vmem_limit_bytes=67043328
        ),
    )(acts, grad_out, projector, moment, second)


def shards(acts, grad_out, projector, moment, second):
    low, new_projector, update = fused(acts.T, grad_out, projector, moment, second)
    proj_grad = low.astype(F32)
    moment_f = 0.9 * moment.astype(F32) + 0.1 * proj_grad
    second_f = 0.95 * second.astype(F32) + 0.05 * proj_grad * proj_grad
    row_count = D // lax.axis_size("dp")
    return new_projector, moment_f.astype(BF16), second_f.astype(BF16), update[:row_count]


def solution(mesh):
    in_specs = (
        P("dp", "shard"),
        P("dp", "shard"),
        P("shard", None),
        P(None, "shard"),
        P(None, "shard"),
    )
    out_specs = (P("shard", None), P(None, "shard"), P(None, "shard"), P("dp", "shard"))
    return jax.shard_map(shards, mesh=mesh, in_specs=in_specs, out_specs=out_specs, check_vma=False)
```

```python
import jax
import jax.numpy as jnp
from jax import lax
from jax.experimental import pallas as pl
from jax.experimental.pallas import tpu as pltpu
from jax.sharding import PartitionSpec as P

D = 1792
F = 3584
RANK = 256
NX, NY, NZ = 4, 8, 8
CHUNKS = 2
CHUNK = RANK // CHUNKS
HALF = CHUNK // 2
STRIP = HALF // NY
MESH = pl.DeviceIdType.MESH
F32 = jnp.float32
BF16 = jnp.bfloat16


def dot_nt(a, b, precision=None):
    return lax.dot_general(
        a, b, (((1,), (1,)), ((), ())), precision=precision, preferred_element_type=F32
    )


def dot_nn(a, b, precision=None):
    return lax.dot_general(
        a, b, (((1,), (0,)), ((), ())), precision=precision, preferred_element_type=F32
    )


def step_kernel(
    acts_hbm, grad_hbm, proj_hbm, moment_hbm, second_hbm,
    low_hbm, new_out, update_out,
    acts, grad, proj, moment, second, pt, rows, low,
    xs, xr, xg, ys, yr, yg,
    h1, s1, r1, q1, g1,
    h2, s2, r2, q2, g2,
    er, ef, gr, gf,
    load, xsend, xrecv, dsend, drecv,
):
    dp, x = lax.axis_index("dp"), lax.axis_index("shard")
    core = lax.rem(dp, 2)
    z = lax.rem(lax.div(dp, 2), NZ)
    y = lax.div(dp, 2 * NZ)
    other = 1 - core
    pos1 = y * other + z * core
    pos2 = y * core + z * other

    def on_x(j):
        return (dp, lax.rem(x + j, NX))

    def on_first(j):
        return ((lax.rem(y + j * other, NY) * NZ + lax.rem(z + j * core, NZ)) * 2 + core, x)

    def on_second(j):
        return ((lax.rem(y + j * core, NY) * NZ + lax.rem(z + j * other, NZ)) * 2 + core, x)

    def on_cross(j, axis):
        row = lax.rem(y + j * (1 - axis), NY)
        return ((row * NZ + lax.rem(z + j * axis, NZ)) * 2 + other, x)

    partner = (dp + 1 - 2 * core, x)
    x_order = (2, 1, 3)
    order = (4, 3, 5, 2, 6, 1, 7)
    pending = []

    def send(src, dst, send_sem, recv_sem, device):
        copy = pltpu.make_async_remote_copy(
            src_ref=src, dst_ref=dst, send_sem=send_sem, recv_sem=recv_sem,
            device_id=device, device_id_type=MESH,
        )
        copy.start()
        pending.append(copy)
        return copy

    barrier = pltpu.get_barrier_semaphore()
    peers = [on_x(j) for j in x_order] + [partner]
    peers += [on_first(j) for j in order] + [on_second(j) for j in order]
    peers += [on_cross(j, axis) for axis in (core, other) for j in order]
    for peer in peers:
        pl.semaphore_signal(barrier, inc=1, device_id=peer, device_id_type=MESH)

    loads = []
    pairs = ((proj_hbm, proj), (acts_hbm, acts), (grad_hbm, grad), (moment_hbm, moment), (second_hbm, second))
    for i, (source, target) in enumerate(pairs):
        loads.append(pltpu.make_async_copy(source, target, load.at[i]))
        loads[-1].start()

    def eye(n, m, shift):
        r = lax.broadcasted_iota(jnp.int32, (n, m), 0)
        c = lax.broadcasted_iota(jnp.int32, (n, m), 1)
        return jnp.where(r + shift == c, 1.0, 0.0)

    own_block = D // NX
    count = D // (NY * NZ * 2)
    quarter = grad.shape[0] // NX
    loads[0].wait()
    pt[...] = dot_nt(eye(RANK, RANK, 0).astype(BF16), proj[...]).astype(BF16)
    first_row = lax.rem(dp, own_block // count) * count
    rows[x] = dot_nn(eye(16, own_block, first_row).astype(BF16), proj[...]).astype(BF16)
    loads[1].wait()

    def span(q):
        return pl.ds(pl.multiple_of(q * quarter, quarter), quarter)

    done = {}

    def once(name, action):
        if name not in done:
            done[name] = action()

    def x_exchange(slot, term, finish, s, r, g):
        copies = []
        for j in x_order:
            s[j - 1] = term(lax.rem(x + j, NX)).astype(BF16)
            once("barrier", lambda: pl.semaphore_wait(barrier, len(peers)))
            k = slot + j - 1
            copies.append(send(s.at[j - 1], r.at[j - 1], xsend.at[k], xrecv.at[k], on_x(j)))
        total = term(x)
        yield
        for copy, j in zip(copies, x_order):
            copy.wait_recv()
            total = total + r[j - 1].astype(F32)
        g[x] = finish(total).astype(BF16)
        gathers = {}
        for j in x_order:
            k = slot + 3 + j - 1
            gathers[j] = send(g.at[x], g.at[x], xsend.at[k], xrecv.at[k], on_x(j))
        return gathers

    def x_contract(g, gathers, term):
        total = term(g[x], x)
        yield
        for j in (1, 3, 2):
            gathers[j].wait_recv()
            q = lax.rem(x + NX - j, NX)
            total = total + term(g[q], q)
        return total

    def plane_sum(slot, local, h, s, r, q, g):
        for half in range(2):
            for i in range(NY):
                first = half * HALF + i * STRIP
                strip = local[first:first + STRIP]
                s[half, i] = strip.astype(BF16)
                h[half, i] = strip
        copies = []
        at = y * core + z * other
        for j in order:
            k = slot + j
            source = s.at[core, lax.rem(pos1 + j, NY)]
            copies.append(send(source, r.at[j - 1], dsend.at[k], drecv.at[k], on_first(j)))
            k = slot + 22 + j
            source = s.at[other, lax.rem(at + j, NY)]
            copies.append(send(source, r.at[6 + j], dsend.at[k], drecv.at[k], on_cross(j, other)))
        k = slot
        copies.append(send(s.at[other, at], r.at[14], dsend.at[k], drecv.at[k], partner))
        yield
        for copy in copies:
            copy.wait_recv()
        total = h[core, pos1]
        for j in range(15):
            total = total + r[j].astype(F32)
        q[pos2] = total.astype(q.dtype)
        copies = []
        for j in order:
            k = slot + 7 + j
            copies.append(send(q.at[pos2], q.at[pos2], dsend.at[k], drecv.at[k], on_second(j)))
        yield
        for copy in copies:
            copy.wait_recv()
        total = q[0].astype(F32)
        for j in range(1, NZ):
            total = total + q[j].astype(F32)
        g[core, pos1] = total.astype(g.dtype)
        copies = []
        for j in order:
            k = slot + 14 + j
            copies.append(
                send(g.at[core, pos1], g.at[core, pos1], dsend.at[k], drecv.at[k], on_first(j))
            )
        yield
        for copy in copies:
            copy.wait_recv()
        swap = send(g.at[core], g.at[core], dsend.at[slot + 22], drecv.at[slot + 22], partner)
        yield
        swap.wait_recv()

    inv_width = 1.0 / D**0.5
    row_copies = []
    updates = []

    def send_rows():
        for j in x_order:
            k = 12 * CHUNKS + j - 1
            row_copies.append(send(rows.at[x], rows.at[x], xsend.at[k], xrecv.at[k], on_x(j)))

    def wait_rows():
        for copy in row_copies:
            copy.wait_recv()

    def wait_states():
        loads[3].wait()
        loads[4].wait()

    early = []

    def block(i):
        return g2[i].reshape(CHUNK, own_block).astype(BF16)

    def spread(slot, ref):
        return [
            send(ref.at[x], ref.at[x], xsend.at[slot + j - 1], xrecv.at[slot + j - 1], on_x(j))
            for j in x_order
        ]

    def chain(i):
        part = slice(i * CHUNK, (i + 1) * CHUNK)
        gathers = yield from x_exchange(
            12 * i, lambda q: dot_nn(pt[part, :], acts[:, span(q)]), lambda v: v * inv_width,
            xs.at[i], xr.at[i], xg.at[i],
        )
        once("rows", send_rows)
        once("grad", loads[2].wait)
        local = yield from x_contract(xg.at[i], gathers, lambda v, q: dot_nn(v, grad[span(q), :]))
        bufs = [b.at[i] for b in (h1, s1, r1, q1, g1)]
        yield from plane_sum(76 * i, local, *bufs)
        low[i] = g1[i].reshape(CHUNK, grad.shape[1])
        store = pltpu.make_async_copy(low.at[i], low_hbm.at[pl.ds(i * CHUNK, CHUNK), :], load.at[5 + i])
        store.start()
        exchange = x_exchange(
            12 * i + 6, lambda q: dot_nt(low[i], grad[span(q), :]), lambda v: v,
            ys.at[i], yr.at[i], yg.at[i],
        )
        next(exchange)
        once("states", wait_states)
        once("wait_rows", wait_rows)
        step = low[i].astype(F32)
        moment_f = 0.9 * moment[part, :].astype(F32) + 0.1 * step
        second_f = 0.95 * second[part, :].astype(F32) + 0.05 * step * step
        first_fix = 1.0 - 0.9**20
        second_fix = 1.0 - 0.95**20
        direction = (moment_f / first_fix / (jnp.sqrt(second_f / second_fix) + 1e-08)).astype(BF16)
        mine = rows[lax.div(dp, own_block // count)]
        updates.append(dot_nn(mine[:, part], direction))
        yield
        gathers = yield from exchange
        local = yield from x_contract(yg.at[i], gathers, lambda v, q: dot_nt(v, acts[:, span(q)]))
        bufs = [b.at[i] for b in (h2, s2, r2, q2, g2)]
        yield from plane_sum(76 * i + 38, local, *bufs)
        store.wait()
        if i == 0:
            strip = g2[0, core].reshape(HALF, own_block).astype(BF16)
            er[x] = dot_nt(strip, block(0)).astype(BF16)
            early.extend(spread(24 + 3, er))

    live = [chain(i) for i in range(CHUNKS)]
    while live:
        for one in list(live):
            try:
                next(one)
            except StopIteration:
                live.remove(one)

    sub = g2[...].reshape(RANK, own_block)
    gr[x] = dot_nt(block(core), block(1)).astype(BF16)
    copies = spread(24 + 6, gr)
    turned = sub.T
    low_turned = turned.astype(BF16)
    update_out[...] = (sum(updates) / RANK**0.5).astype(BF16)
    for copy in early + copies:
        copy.wait_recv()

    def gathered(ref):
        total = ref[0].astype(F32)
        for j in range(1, NX):
            total = total + ref[j].astype(F32)
        return total

    ef[core] = gathered(er)
    gf[core] = gathered(gr)
    k = 76 * CHUNKS
    swaps = [
        send(ef.at[core], ef.at[core], dsend.at[k], drecv.at[k], partner),
        send(gf.at[core], gf.at[core], dsend.at[k + 1], drecv.at[k + 1], partner),
    ]
    for copy in swaps:
        copy.wait_recv()
    cross_gram = gf[0]
    upper = jnp.concatenate([ef[...].reshape(CHUNK, CHUNK), cross_gram], axis=1)
    lower = jnp.concatenate([cross_gram.T, gf[1]], axis=1)
    gram = jnp.concatenate([upper, lower], axis=0)
    trace = jnp.sum(gram * eye(RANK, RANK, 0), axis=(0, 1), keepdims=True)
    mean_square = trace / (D * RANK) + 1e-06
    cubic = dot_nn(low_turned, gram.astype(BF16))
    new = (1.5 * turned - 0.5 * cubic / (mean_square * D)) / jnp.sqrt(mean_square)
    new_out[...] = new.astype(BF16)
    for copy in pending:
        copy.wait_send()


def fused(acts, grad_out, projector, moment, second):
    own, tokens = acts.shape
    wide = grad_out.shape[1]
    quarter = tokens // NX

    def plane(width, part, gathered):
        return [
            pltpu.VMEM((CHUNKS, 2, NY, STRIP, width), F32),
            pltpu.VMEM((CHUNKS, 2, NY, STRIP, width), BF16),
            pltpu.VMEM((CHUNKS, 2 * NY - 1, STRIP, width), BF16),
            pltpu.VMEM((CHUNKS, NZ, STRIP, width), part),
            pltpu.VMEM((CHUNKS, 2, NY, STRIP, width), gathered),
        ]

    def cross():
        return [
            pltpu.VMEM((CHUNKS, NX - 1, CHUNK, quarter), BF16),
            pltpu.VMEM((CHUNKS, NX - 1, CHUNK, quarter), BF16),
            pltpu.VMEM((CHUNKS, NX, CHUNK, quarter), BF16),
        ]

    vmem = pl.BlockSpec(memory_space=pltpu.VMEM)
    anywhere = pl.BlockSpec(memory_space=pl.ANY)
    return pl.pallas_call(
        step_kernel,
        out_shape=(
            jax.ShapeDtypeStruct((RANK, wide), BF16),
            jax.ShapeDtypeStruct((own, RANK), BF16),
            jax.ShapeDtypeStruct((16, wide), BF16),
        ),
        in_specs=[anywhere] * 5,
        out_specs=(anywhere, vmem, vmem),
        scratch_shapes=[
            pltpu.VMEM((own, tokens), BF16),
            pltpu.VMEM((tokens, wide), BF16),
            pltpu.VMEM((own, RANK), BF16),
            pltpu.VMEM((RANK, wide), BF16),
            pltpu.VMEM((RANK, wide), BF16),
            pltpu.VMEM((RANK, own), BF16),
            pltpu.VMEM((NX, 16, RANK), BF16),
            pltpu.VMEM((CHUNKS, CHUNK, wide), BF16),
            *cross(),
            *cross(),
            *plane(wide, BF16, BF16),
            *plane(own, F32, F32),
            pltpu.VMEM((NX, HALF, CHUNK), BF16),
            pltpu.VMEM((2, HALF, CHUNK), F32),
            pltpu.VMEM((NX, CHUNK, CHUNK), BF16),
            pltpu.VMEM((2, CHUNK, CHUNK), F32),
            pltpu.SemaphoreType.DMA((5 + CHUNKS,)),
            pltpu.SemaphoreType.DMA((12 * CHUNKS + 9,)),
            pltpu.SemaphoreType.DMA((12 * CHUNKS + 9,)),
            pltpu.SemaphoreType.DMA((76 * CHUNKS + 2,)),
            pltpu.SemaphoreType.DMA((76 * CHUNKS + 2,)),
        ],
        compiler_params=pltpu.CompilerParams(
            collective_id=0, has_side_effects=True, vmem_limit_bytes=67043328
        ),
    )(acts, grad_out, projector, moment, second)


def shards(acts, grad_out, projector, moment, second):
    low, new_projector, update = fused(acts.T, grad_out, projector, moment, second)
    proj_grad = low.astype(F32)
    moment_f = 0.9 * moment.astype(F32) + 0.1 * proj_grad
    second_f = 0.95 * second.astype(F32) + 0.05 * proj_grad * proj_grad
    row_count = D // lax.axis_size("dp")
    return new_projector, moment_f.astype(BF16), second_f.astype(BF16), update[:row_count]


def solution(mesh):
    in_specs = (
        P("dp", "shard"),
        P("dp", "shard"),
        P("shard", None),
        P(None, "shard"),
        P(None, "shard"),
    )
    out_specs = (P("shard", None), P(None, "shard"), P(None, "shard"), P("dp", "shard"))
    return jax.shard_map(shards, mesh=mesh, in_specs=in_specs, out_specs=out_specs, check_vma=False)
```
